32 devices in a mesh: space: 4 (over y, x), slot: 8 (over z, core).
Axes of the slice: x: 2, y: 2, z: 4, core: 2. Of those that a mesh axis runs over, the one named last changes fastest.
Arguments:
- control: bfloat16 [1536, 1024], P('slot', 'space'), may hold values from -6 to 6
- block_lists: int32 [32, 2], P('space'), may hold values from 0 to 7, all different within a row; in each aligned block of 8 rows (0 to 7, 8 to 15, ...) at most 2 rows name the same one
- loc_tiles: bfloat16 [32, 2, 128, 128], P('space'), may hold values from -0.375 to 0.375
- ensemble: bfloat16 [8, 1536, 4096], P('slot', None, 'space'), may hold values from -2.5 to 2.5
- obs_col: int32 [8, 8192], P('slot', 'space'), may hold values from 0 to 4095, as said below
- obs_wts: float32 [8, 48, 8192], P('slot', None, 'space'), may hold values from -0.875 to 0.875
- innovation: float32 [8, 8192], P('slot', 'space'), may hold values from -6 to 6
- inv_error: float32 [8, 8192], P('slot', 'space'), may hold values from 1 to 16
Outputs:
- first_grad: float32 [1536, 1024], P('slot', 'space')
- second_grad: float32 [1536, 1024], P('slot', 'space')
The draws below stay inside these ranges and needn't reach their ends.
Inputs may be any that keep to these rules, and one draw needn't show every extreme that they name: `block_lists`: each grid block lists 2 different control blocks; among the grid blocks of one space index no control block is listed more than twice. `obs_col`: observation j lies in grid columns (j // 2048) * 8 * 128 to that plus 8 * 128 - 1.
All inputs are finite; a program needn't handle non-finite values.
Results may differ from the reference program's by a relative error of at most 0.0003.
Values may be sent and summed in bfloat16 or wider, within the bound.
A program may use at most 64 MiB of HBM per device.

```python
import math
import jax
import jax.numpy as jnp
import numpy as np
from jax import lax

LEV = 48
MEMBERS = 32
BLOCK = 128
K = 2
NOBS_DEV = 2048
GB_DEV = 8
SLOTS = 8
COLS = 1536
NCB = 8
NC = 1024
NGB = 32
NG = 4096
NOBS = 8192


def draw_obs_col(key, part):
    offsets = jax.random.randint(key, (SLOTS, NOBS), 0, GB_DEV * BLOCK, dtype=jnp.int32)
    offsets = offsets.at[:, 0].set(0)
    offsets = offsets.at[:, NOBS - 1].set(GB_DEV * BLOCK - 1)
    owner = jnp.arange(NOBS, dtype=jnp.int32) // NOBS_DEV
    return (offsets + owner[None, :] * (GB_DEV * BLOCK)).astype(jnp.int32)


def shard_levels(own_key, dims, pieces, least, largest):
    def one(position, parts):
        draws = jax.random.uniform(jax.random.fold_in(jax.random.fold_in(own_key, 6), position), (parts,), jnp.float32, least / len(pieces), largest / len(pieces))
        return jnp.repeat(jnp.exp(draws), dims[position] // parts).reshape((-1,) + (1,) * (len(dims) - position - 1))

    factor_of = one(*pieces[0])
    for cut in pieces[1:]:
        factor_of = factor_of * one(*cut)
    return factor_of


def shared_out(own_key, own, number, rows, amount, top, bound, skew):
    ranking = jax.random.permutation(own_key, amount)
    heavy_load, ordinary = load_shares(amount, rows * top, bound, skew, True), load_shares(amount, rows * top, bound, skew, False)
    places = jnp.arange(amount)

    def named(lengths, rotation):
        used = int((lengths > 0).sum())
        fixed = max(1, used // 4)
        passed = fixed + (places - fixed + rotation * (used - fixed)) % max(1, amount - fixed)
        return jnp.zeros((amount,), jnp.int32).at[ranking[jnp.where(places < fixed, places, passed)]].set(jnp.asarray(lengths, jnp.int32))

    lengths = jnp.where(number % 4 == 0, named(heavy_load, number // 4), named(ordinary, number - number // 4 - 1))
    mixed = jax.random.permutation(jax.random.fold_in(own, 3), amount)
    donor, taker = mixed[0:amount // 2 * 2:2], mixed[1:amount // 2 * 2:2]
    margin = jnp.minimum(lengths[donor] - 1, bound - lengths[taker]) // 2
    margin = jnp.where((donor == ranking[0]) | (taker == ranking[0]) | (lengths[taker] == 0), 0, jnp.maximum(margin, 0))
    passed = jax.random.randint(jax.random.fold_in(own, 4), (amount // 2,), 0, 1 << 20) % (margin + 1)
    lengths = lengths.at[donor].add(-passed).at[taker].add(passed)
    labels = jnp.searchsorted(jnp.cumsum(lengths), jnp.arange(rows * top), side="right").astype(jnp.int32)
    grid = labels.reshape(top, rows).T
    grid = grid[jax.random.permutation(jax.random.fold_in(own, 1), rows)]
    rotation = jax.random.randint(jax.random.fold_in(own, 2), (rows, 1), 0, top)
    return jnp.take_along_axis(grid, (jnp.arange(top)[None, :] + rotation) % top, axis=1)


def load_shares(amount, total, reach, skew, full):
    loads = [(1 << 20) // math.isqrt(grade ** skew) + 1 for grade in range(1, amount + 1)]
    largest = reach if full else min(reach, max(-(-total // amount), total * loads[0] // sum(loads)))
    least = 1 if total - largest >= amount - 1 else 0
    given, surplus = [largest] + [least] * (amount - 1), total - largest - least * (amount - 1)
    while surplus > 0:
        free = [i for i in range(1, amount) if given[i] < largest] or [i for i in range(1, amount) if given[i] < reach]
        mass, remaining = sum([loads[i] for i in free]), surplus
        for i in free:
            more = min(reach - given[i], max(1, remaining * loads[i] // mass), surplus)
            given[i] = given[i] + more
            surplus = surplus - more
    return np.array(given)


def gaussian(own_key, shape, deviation, limit, split=(), kind=jnp.bfloat16):
    drawn = deviation * jax.random.normal(own_key, shape, jnp.float32)
    if split:
        drawn = drawn * shard_levels(own_key, shape, split, -0.22, 0.18)
    return jnp.clip(drawn, -limit, limit).astype(kind)


def setup_inputs(seed: int = 0) -> dict:
    keys = jax.random.split(jax.random.key(seed), 9)
    control = gaussian(keys[0], (COLS, NC), 1.0, 6.0, ((0, 8), (1, 4)))
    block_lists_keys = jax.random.split(jax.random.fold_in(keys[1], 1), NGB // GB_DEV)
    block_lists_turns = jax.random.permutation(jax.random.fold_in(keys[1], 3), NGB // GB_DEV)
    block_lists = jax.vmap(lambda own, number: shared_out(jax.random.fold_in(keys[1], 2), own, number, GB_DEV, NCB, K, 2, 2))(block_lists_keys, block_lists_turns).reshape((NGB, K))
    loc_tiles = gaussian(keys[2], (NGB, K, BLOCK, BLOCK), (BLOCK * K) ** -0.5, 0.375, ((0, 4),))
    ensemble = gaussian(keys[3], (SLOTS, COLS, NG), 0.18, 2.5, ((0, 8), (2, 4)))
    obs_col = draw_obs_col(jax.random.fold_in(keys[8], 71), 0)
    obs_wts = gaussian(keys[5], (SLOTS, LEV, NOBS), LEV ** -0.5, 0.875, ((0, 8), (2, 4)), jnp.float32)
    innovation = gaussian(keys[6], (SLOTS, NOBS), 1.0, 6.0, ((0, 8), (1, 4)), jnp.float32)
    inv_error = jnp.clip(jnp.exp(math.log(16.0) - 2.7725887 * jax.random.uniform(keys[7], (SLOTS, NOBS), jnp.float32) ** shard_levels(keys[7], (SLOTS, NOBS), ((0, 8), (1, 4)), -0.2, 0.2)), 1.0, 16.0)
    return dict(control=control, block_lists=block_lists, loc_tiles=loc_tiles, ensemble=ensemble, obs_col=obs_col, obs_wts=obs_wts, innovation=innovation, inv_error=inv_error)


descent_step = 0.5


def localize(control, block_lists, loc_tiles):
    picked = control.astype(jnp.float32).reshape(COLS, NCB, BLOCK)[:, block_lists.reshape(-1), :]
    tiles_flat = loc_tiles.reshape(NGB * K, BLOCK, BLOCK).astype(jnp.float32)
    products = jnp.einsum("crj,rij->cri", picked, tiles_flat, precision=lax.Precision.HIGHEST)
    return products.reshape(COLS, NGB, K, BLOCK).sum(axis=2).reshape(COLS, NG)


def adjoint(forcing, block_lists, loc_tiles):
    grid_cells = forcing.reshape(COLS, NGB, BLOCK)
    products = jnp.einsum("cgi,gkij->cgkj", grid_cells, loc_tiles.astype(jnp.float32), precision=lax.Precision.HIGHEST)
    selector = (block_lists.reshape(-1)[:, None] == jnp.arange(NCB, dtype=jnp.int32)[None, :]).astype(jnp.float32)
    summed = jnp.einsum("rb,crj->cbj", selector, products.reshape(COLS, NGB * K, BLOCK), precision=lax.Precision.HIGHEST)
    return summed.reshape(COLS, NC)


def gradient(control, block_lists, loc_tiles, ensemble, obs_col, obs_wts, innovation, inv_error):
    updates = localize(control, block_lists, loc_tiles).reshape(MEMBERS, LEV, NG)

    def slot_step(running, slot_items):
        members, columns, weights, observed, inverse = slot_items
        spread = members.astype(jnp.float32).reshape(MEMBERS, LEV, NG)
        increment = jnp.sum(spread * updates, axis=0)
        modelled = jnp.sum(weights * increment[:, columns], axis=0)
        residual = inverse * (modelled - observed)
        adjoint_obs = jnp.zeros((LEV, NG), jnp.float32).at[:, columns].add(weights * residual[None, :])
        return running + (spread * adjoint_obs[None]).reshape(COLS, NG), None

    forcing, unused = lax.scan(slot_step, jnp.zeros((COLS, NG), jnp.float32), (ensemble, obs_col, obs_wts, innovation, inv_error))
    return control.astype(jnp.float32) + adjoint(forcing, block_lists, loc_tiles)


def reference(control, block_lists, loc_tiles, ensemble, obs_col, obs_wts, innovation, inv_error):
    first_grad = gradient(control, block_lists, loc_tiles, ensemble, obs_col, obs_wts, innovation, inv_error)
    stepped = control.astype(jnp.float32) - descent_step * first_grad
    second_grad = gradient(stepped, block_lists, loc_tiles, ensemble, obs_col, obs_wts, innovation, inv_error)
    return first_grad, second_grad
```

```python
import jax
import jax.numpy as jnp
from jax import lax
from jax.sharding import PartitionSpec as P

LEV = 48
BLOCK = 128
K = 2
descent_step = 0.5
F32 = jnp.float32
BF16 = jnp.bfloat16


def parts(x):
    high = lax.reduce_precision(x, 8, 7)
    low = lax.reduce_precision(x - high, 8, 7)
    return high.astype(BF16), low.astype(BF16)


def mm(a, b, dims):
    return lax.dot_general(a, b, (dims, ((), ())), preferred_element_type=F32)


def mm2(x, b, dims):
    high, low = parts(x)
    return mm(high, b, dims) + mm(low, b, dims)


def per_device(control, block_lists, loc_tiles, ensemble, obs_col, obs_wts, innovation, inv_error):
    rows = control.shape[0]
    cells = ensemble.shape[2]
    slots = lax.axis_size("slot")
    blocks = control.shape[1] // BLOCK * lax.axis_size("space")
    local_cols = obs_col[0] - lax.axis_index("space") * cells
    pick = (jnp.arange(cells, dtype=jnp.int32)[:, None] == local_cols[None, :]).astype(BF16)
    weights, inverse, observed = obs_wts[0], inv_error[0], innovation[0]
    spread = lax.all_to_all(ensemble.reshape(slots, rows, cells), "slot", 0, 0)
    spread = spread.reshape(slots, rows // LEV, LEV, cells)
    chosen = block_lists[:, :, None] == jnp.arange(blocks, dtype=jnp.int32)
    dense = jnp.sum(
        jnp.where(chosen[..., None, None], loc_tiles[:, :, None], 0), axis=1, dtype=BF16
    )
    dense = dense.transpose(0, 2, 1, 3).reshape(cells, blocks * BLOCK)

    def gradient(updates, base):
        updates = updates.reshape(1, rows // LEV, LEV, cells)
        partial = jnp.sum(spread.astype(F32) * updates, axis=1)
        increment = lax.psum_scatter(partial, "slot", scatter_dimension=0, tiled=True)[0]
        seen = mm2(increment, pick, ((1,), (0,)))
        residual = inverse * (jnp.sum(weights * seen, axis=0) - observed)
        adjoint = mm2(weights * residual[None], pick, ((1,), (1,)))
        everyone = lax.all_gather(adjoint, "slot", axis=0)
        forcing = jnp.sum(spread.astype(F32) * everyone[:, None], axis=0).reshape(rows, cells)
        term = mm2(forcing, dense, ((1,), (0,)))
        return base + lax.psum_scatter(term, "space", scatter_dimension=1, tiled=True)

    whole = lax.all_gather(control, "space", axis=1, tiled=True)
    wide = control.astype(F32)
    first = gradient(mm(whole, dense, ((1,), (1,))), wide)
    stepped = wide - descent_step * first
    whole = lax.all_gather(stepped, "space", axis=1, tiled=True)
    second = gradient(mm2(whole, dense, ((1,), (1,))), stepped)
    return first, second


def solution(mesh):
    placed = (
        P("slot", "space"),
        P("space", None),
        P("space", None, None, None),
        P("slot", None, "space"),
        P("slot", "space"),
        P("slot", None, "space"),
        P("slot", "space"),
        P("slot", "space"),
    )
    return jax.shard_map(
        per_device,
        mesh=mesh,
        in_specs=placed,
        out_specs=(P("slot", "space"), P("slot", "space")),
        check_vma=False,
    )
```

```python
import functools

import jax
import jax.numpy as jnp
from jax import lax
from jax.experimental import pallas as pl
from jax.experimental.pallas import tpu as pltpu
from jax.sharding import PartitionSpec as P

LEV = 48
BLOCK = 128
CORES = 2
CHUNK = 256
OBS_CHUNK = 512
descent_step = 0.5
F32 = jnp.float32
BF16 = jnp.bfloat16
MESH = pl.DeviceIdType.MESH


def halves(x):
    high = x.astype(BF16)
    return high, (x - high.astype(F32)).astype(BF16)


def dot(a, b):
    return lax.dot_general(a, b, (((1,), (0,)), ((), ())), preferred_element_type=F32)


def dot_t(a, b):
    return lax.dot_general(a, b, (((1,), (1,)), ((), ())), preferred_element_type=F32)


def kernel(
    spaces, slots,
    control, lists, tiles, ensemble, cols, wts, innovation, inverse,
    first_ref, second_ref,
    ens, dense, pick, updates, adjsum, forced, out_a, in_a, sums, in_b, adj, term, term_in, step_src,
    ctl_in, step_in,
    local_sem, ens_s, ens_r, a_s, a_r, b_s, b_r, c_s, c_r, d_s, d_r, g_s, g_r, t_s, t_r,
):
    rows, width = control.shape
    cells = ensemble.shape[2]
    nobs = cols.shape[1]
    chips = slots // CORES
    members = rows // LEV
    me = lax.axis_index("space")
    slot = lax.axis_index("slot")
    z, core = slot // CORES, lax.rem(slot, CORES)
    sibling = slot + 1 - 2 * core

    def slot_at(dz, dk):
        zz = lax.rem(z + dz + chips, chips)
        return zz * CORES + (core if dk == 0 else 1 - core)

    def space_at(d):
        return lax.rem(me + d + spaces, spaces)

    barrier = pltpu.get_barrier_semaphore()
    for dz in range(chips):
        for dk in range(CORES):
            if dz or dk:
                pl.semaphore_signal(
                    barrier, inc=1, device_id={"slot": slot_at(dz, dk)}, device_id_type=MESH
                )
    for d in range(1, spaces):
        pl.semaphore_signal(barrier, inc=1, device_id={"space": space_at(d)}, device_id_type=MESH)
    pl.semaphore_wait(barrier, slots - 1 + spaces - 1)

    def send(src, dst, ssem, rsem, where):
        copy = pltpu.make_async_remote_copy(
            src_ref=src, dst_ref=dst, send_sem=ssem, recv_sem=rsem,
            device_id=where, device_id_type=MESH,
        )
        copy.start()
        return copy

    gathers = [
        send(control, ctl_in.at[d - 1], g_s.at[0, d - 1], g_r.at[0, d - 1], {"space": space_at(d)})
        for d in range(1, spaces)
    ]
    moved = {}
    for dz in sorted(range(chips), key=lambda v: -min(v, chips - v)):
        for dk in range(CORES):
            if dz or dk:
                rel = dz * CORES + dk
                to = slot_at(dz, dk)
                moved[rel] = send(
                    ensemble.at[0, pl.ds(pl.multiple_of(to * rows, rows), rows)],
                    ens.at[rel], ens_s.at[rel - 1], ens_r.at[rel - 1], {"slot": to},
                )
    own = pltpu.make_async_copy(
        ensemble.at[0, pl.ds(pl.multiple_of(slot * rows, rows), rows)], ens.at[0], local_sem
    )
    own.start()

    per = width // BLOCK

    def build_dense(g, carry):
        one = lists[g, 0]
        two = lists[g, 1]
        tile_one = tiles[g, 0].astype(F32)
        tile_two = tiles[g, 1].astype(F32)
        at = pl.ds(pl.multiple_of(g * BLOCK, BLOCK), BLOCK)
        for b in range(spaces * per):
            mask_one = jnp.where(one == b, 1.0, 0.0)
            mask_two = jnp.where(two == b, 1.0, 0.0)
            value = tile_one * mask_one + tile_two * mask_two
            dense[b // per, at, (b % per) * BLOCK : (b % per + 1) * BLOCK] = value.astype(BF16)
        return carry

    lax.fori_loop(0, cells // BLOCK, build_dense, 0)

    first_cell = me * cells

    def build_pick(q, carry):
        line = cols[:, pl.ds(pl.multiple_of(q * OBS_CHUNK, OBS_CHUNK), OBS_CHUNK)] - first_cell

        def band(r, inner):
            rowid = lax.broadcasted_iota(jnp.int32, (BLOCK, OBS_CHUNK), 0) + r * BLOCK
            hot = jnp.where(rowid == line, 1.0, 0.0).astype(BF16)
            pick[q, pl.ds(pl.multiple_of(r * BLOCK, BLOCK), BLOCK)] = hot
            return inner

        return lax.fori_loop(0, cells // BLOCK, band, carry)

    lax.fori_loop(0, nobs // OBS_CHUNK, build_pick, 0)

    def chunks(body):
        def run(c, carry):
            body(pl.ds(pl.multiple_of(c * CHUNK, CHUNK), CHUNK))
            return carry

        lax.fori_loop(0, cells // CHUNK, run, 0)

    def project(rel, at):
        total = None
        for m in range(members):
            lev = slice(m * LEV, (m + 1) * LEV)
            value = ens[rel, lev, at].astype(F32) * updates[lev, at]
            total = value if total is None else total + value
        return total

    def gradient(i, base):
        sent = []
        copies_a = {}
        for dz in list(range(1, chips)) + [0]:
            rel = dz * CORES + 1
            if i == 0:
                moved[rel].wait_recv()

            def fill(at, rel=rel, dz=dz):
                out_a[i, dz, :, at] = project(rel, at)

            chunks(fill)
            copies_a[dz] = send(
                out_a.at[i, dz], in_a.at[i, dz], a_s.at[i, dz], a_r.at[i, dz], {"slot": sibling}
            )
        copies_b = {}
        for dz in list(range(1, chips)) + [0]:
            rel = dz * CORES
            if i == 0:
                if rel:
                    moved[rel].wait_recv()
                else:
                    own.wait()
            copies_a[dz].wait_recv()

            def fold(at, rel=rel, dz=dz):
                sums[i, dz, :, at] = project(rel, at) + in_a[i, dz, :, at]

            chunks(fold)
            if dz:
                copies_b[dz] = send(
                    sums.at[i, dz], in_b.at[i, dz - 1], b_s.at[i, dz - 1], b_r.at[i, dz - 1],
                    {"slot": slot_at(-dz, 0)},
                )
        for dz in range(1, chips):
            copies_b[dz].wait_recv()
        increment = sums[i, 0]
        for dz in range(1, chips):
            increment = increment + in_b[i, dz - 1]
        high, low = halves(increment)
        pair = jnp.concatenate([high, low], axis=0)
        adjsum[...] = jnp.zeros_like(adjsum)

        def observe(q, carry):
            at = pl.ds(pl.multiple_of(q * OBS_CHUNK, OBS_CHUNK), OBS_CHUNK)
            table = pick[q]
            seen = dot(pair, table)
            seen = seen[:LEV] + seen[LEV:]
            w = wts[0, :, at]
            modelled = jnp.sum(w * seen, axis=0, keepdims=True)
            residual = inverse[:, at] * (modelled - innovation[:, at])
            up, down = halves(w * residual)
            back = dot_t(jnp.concatenate([up, down], axis=0), table)
            adjsum[...] += back[:LEV] + back[LEV:]
            return carry

        lax.fori_loop(0, nobs // OBS_CHUNK, observe, 0)
        adj[i, 0] = adjsum[...]
        copies_c = {}
        for dz in list(range(1, chips)):
            copies_c[dz] = send(
                adj.at[i, 0], adj.at[i, dz * CORES], c_s.at[i, dz], c_r.at[i, dz],
                {"slot": slot_at(dz, 0)},
            )
        copies_c[0] = send(
            adj.at[i, 0], adj.at[i, 1], c_s.at[i, 0], c_r.at[i, 0], {"slot": sibling}
        )
        copies_d = {}
        for dz in range(1, chips):
            copies_c[dz].wait_recv()
            copies_d[dz] = send(
                adj.at[i, dz * CORES], adj.at[i, dz * CORES + 1], d_s.at[i, dz - 1],
                d_r.at[i, dz - 1], {"slot": sibling},
            )
        copies_c[0].wait_recv()
        for dz in range(1, chips):
            copies_d[dz].wait_recv()

        def force(at):
            for m in range(members):
                lev = slice(m * LEV, (m + 1) * LEV)
                total = ens[0, lev, at].astype(F32) * adj[i, 0, :, at]
                for rel in range(1, slots):
                    total = total + ens[rel, lev, at].astype(F32) * adj[i, rel, :, at]
                up, down = halves(total)
                forced[lev, at] = up
                forced[rows + m * LEV : rows + (m + 1) * LEV, at] = down

        chunks(force)
        copies_t = []
        for d in range(1, spaces):
            to = space_at(d)
            both = dot(forced[...], dense[to])
            term[i, d - 1] = both[:rows] + both[rows:]
            copies_t.append(
                send(
                    term.at[i, d - 1], term_in.at[i, d - 1], t_s.at[i, d - 1], t_r.at[i, d - 1],
                    {"space": to},
                )
            )
        both = dot(forced[...], dense[me])
        total = base + both[:rows] + both[rows:]
        for d in range(1, spaces):
            copies_t[d - 1].wait_recv()
            total = total + term_in[i, d - 1]
        sent += list(copies_a.values()) + list(copies_b.values()) + list(copies_c.values())
        sent += list(copies_d.values()) + copies_t
        return total, sent

    value = dot_t(control[...], dense[me])
    for d in range(1, spaces):
        gathers[d - 1].wait_recv()
        value = value + dot_t(ctl_in[d - 1], dense[space_at(-d)])
    updates[...] = value
    first, sent_one = gradient(0, control[...].astype(F32))
    first_ref[...] = first
    step_src[...] = control[...].astype(F32) - descent_step * first
    again = [
        send(step_src, step_in.at[d - 1], g_s.at[1, d - 1], g_r.at[1, d - 1], {"space": space_at(d)})
        for d in range(1, spaces)
    ]

    def spread(x, table):
        up, down = halves(x)
        both = dot_t(jnp.concatenate([up, down], axis=0), table)
        return both[:rows] + both[rows:]

    updates[...] = spread(step_src[...], dense[me])
    for d in range(1, spaces):
        again[d - 1].wait_recv()
        updates[...] += spread(step_in[d - 1], dense[space_at(-d)])
    second, sent_two = gradient(1, step_src[...])
    second_ref[...] = second
    for copy in gathers + list(moved.values()) + sent_one + again + sent_two:
        copy.wait_send()


def per_device(control, block_lists, loc_tiles, ensemble, obs_col, obs_wts, innovation, inv_error):
    rows, width = control.shape
    cells = ensemble.shape[2]
    nobs = obs_col.shape[1]
    spaces, slots = lax.axis_size("space"), lax.axis_size("slot")
    chips = slots // CORES
    dma = pltpu.SemaphoreType.DMA
    vmem = pl.BlockSpec(memory_space=pltpu.VMEM)
    out = jax.ShapeDtypeStruct((rows, width), F32)
    return pl.pallas_call(
        functools.partial(kernel, spaces, slots),
        out_shape=(out, out),
        in_specs=[
            vmem, pl.BlockSpec(memory_space=pltpu.SMEM), vmem, pl.BlockSpec(memory_space=pl.ANY),
            vmem, vmem, vmem, vmem,
        ],
        out_specs=(vmem, vmem),
        scratch_shapes=[
            pltpu.VMEM((slots, rows, cells), BF16),
            pltpu.VMEM((spaces, cells, width), BF16),
            pltpu.VMEM((nobs // OBS_CHUNK, cells, OBS_CHUNK), BF16),
            pltpu.VMEM((rows, cells), F32),
            pltpu.VMEM((LEV, cells), F32),
            pltpu.VMEM((2 * rows, cells), BF16),
            pltpu.VMEM((2, chips, LEV, cells), F32),
            pltpu.VMEM((2, chips, LEV, cells), F32),
            pltpu.VMEM((2, chips, LEV, cells), F32),
            pltpu.VMEM((2, chips - 1, LEV, cells), F32),
            pltpu.VMEM((2, slots, LEV, cells), F32),
            pltpu.VMEM((2, spaces - 1, rows, width), F32),
            pltpu.VMEM((2, spaces - 1, rows, width), F32),
            pltpu.VMEM((rows, width), F32),
            pltpu.VMEM((spaces - 1, rows, width), BF16),
            pltpu.VMEM((spaces - 1, rows, width), F32),
            dma, dma((slots - 1,)), dma((slots - 1,)),
            dma((2, chips)), dma((2, chips)),
            dma((2, chips - 1)), dma((2, chips - 1)),
            dma((2, chips)), dma((2, chips)),
            dma((2, chips - 1)), dma((2, chips - 1)),
            dma((2, spaces - 1)), dma((2, spaces - 1)),
            dma((2, spaces - 1)), dma((2, spaces - 1)),
        ],
        compiler_params=pltpu.CompilerParams(
            collective_id=0, has_side_effects=True, vmem_limit_bytes=58 * 1024 * 1024
        ),
        name="envar_gradients",
    )(control, block_lists, loc_tiles, ensemble, obs_col, obs_wts, innovation, inv_error)


def solution(mesh):
    placed = (
        P("slot", "space"),
        P("space", None),
        P("space", None, None, None),
        P("slot", None, "space"),
        P("slot", "space"),
        P("slot", None, "space"),
        P("slot", "space"),
        P("slot", "space"),
    )
    return jax.shard_map(
        per_device,
        mesh=mesh,
        in_specs=placed,
        out_specs=(P("slot", "space"), P("slot", "space")),
        check_vma=False,
    )
```

```python
import functools

import jax
import jax.numpy as jnp
from jax import lax
from jax.experimental import pallas as pl
from jax.experimental.pallas import tpu as pltpu
from jax.sharding import PartitionSpec as P

LEV = 48
BLOCK = 128
CORES = 2
CHUNK = 512
GROUP = 16
OBS_CHUNK = 512
descent_step = 0.5
F32 = jnp.float32
BF16 = jnp.bfloat16
MESH = pl.DeviceIdType.MESH


def halves(x):
    high = x.astype(BF16)
    return high, (x - high.astype(F32)).astype(BF16)


def dot(a, b):
    return lax.dot_general(a, b, (((1,), (0,)), ((), ())), preferred_element_type=F32)


def dot_t(a, b):
    return lax.dot_general(a, b, (((1,), (1,)), ((), ())), preferred_element_type=F32)


def staged(stages, count):
    for tick in range(count + len(stages) - 1):
        for place in reversed(range(len(stages))):
            if 0 <= tick - place < count:
                stages[place](tick - place)


def kernel(
    spaces, slots,
    control, lists, tiles, ensemble, cols, wts, innovation, inverse,
    first_ref, second_ref,
    ens, dense, pick, updates, pair, adjsum, forced, out_a, in_a, sums, in_b, adj, term, term_in,
    base, step, ctl_in, step_in,
    local_sem, ens_s, ens_r, ctl_s, ctl_r, a_s, a_r, b_s, b_r, c_s, c_r, o_s, o_r, d_s, d_r,
    g_s, g_r, t_s, t_r,
):
    rows, width = control.shape
    members, cells = ensemble.shape[1], ensemble.shape[3]
    nobs = cols.shape[1]
    chips = slots // CORES
    part = members * GROUP
    groups = LEV // GROUP
    me = lax.axis_index("space")
    slot = lax.axis_index("slot")
    z, core = slot // CORES, lax.rem(slot, CORES)
    sibling = {"slot": slot + 1 - 2 * core}

    def slot_at(dz, dk):
        zz = lax.rem(z + dz + chips, chips)
        return zz * CORES + (core if dk == 0 else 1 - core)

    def space_at(d):
        return lax.rem(me + d + spaces, spaces)

    barrier = pltpu.get_barrier_semaphore()
    for dz in range(chips):
        for dk in range(CORES):
            if dz or dk:
                pl.semaphore_signal(
                    barrier, inc=1, device_id={"slot": slot_at(dz, dk)}, device_id_type=MESH
                )
    for d in range(1, spaces):
        pl.semaphore_signal(barrier, inc=1, device_id={"space": space_at(d)}, device_id_type=MESH)
    pl.semaphore_wait(barrier, slots - 1 + spaces - 1)

    started = []

    def send(src, dst, ssem, rsem, where):
        copy = pltpu.make_async_remote_copy(
            src_ref=src, dst_ref=dst, send_sem=ssem, recv_sem=rsem,
            device_id=where, device_id_type=MESH,
        )
        copy.start()
        started.append(copy)
        return copy

    gathers = [
        send(control, ctl_in.at[d - 1], ctl_s.at[d - 1], ctl_r.at[d - 1], {"space": space_at(d)})
        for d in range(1, spaces)
    ]
    moved = {}
    for dk in (1, 0):
        for dz in sorted(range(chips), key=lambda v: -min(v, chips - v)):
            if dz or dk:
                rel = dk * chips + dz
                to = slot_at(dz, dk)
                moved[rel] = send(
                    ensemble.at[to], ens.at[rel], ens_s.at[rel - 1], ens_r.at[rel - 1], {"slot": to}
                )
    own = pltpu.make_async_copy(ensemble.at[slot], ens.at[0], local_sem)
    own.start()

    per = width // BLOCK

    def build_dense(g, carry):
        one = lists[g, 0]
        two = lists[g, 1]
        tile_one = tiles[g, 0].astype(F32)
        tile_two = tiles[g, 1].astype(F32)
        at = pl.ds(pl.multiple_of(g * BLOCK, BLOCK), BLOCK)
        for b in range(spaces * per):
            mask_one = jnp.where(one == b, 1.0, 0.0)
            mask_two = jnp.where(two == b, 1.0, 0.0)
            value = tile_one * mask_one + tile_two * mask_two
            dense[b // per, at, (b % per) * BLOCK : (b % per + 1) * BLOCK] = value.astype(BF16)
        return carry

    lax.fori_loop(0, cells // BLOCK, build_dense, 0)

    first_cell = me * cells

    def build_pick(q, carry):
        line = cols[:, pl.ds(pl.multiple_of(q * OBS_CHUNK, OBS_CHUNK), OBS_CHUNK)] - first_cell

        def band(r, inner):
            rowid = lax.broadcasted_iota(jnp.int32, (BLOCK, OBS_CHUNK), 0) + r * BLOCK
            hot = jnp.where(rowid == line, 1.0, 0.0).astype(BF16)
            pick[q, pl.ds(pl.multiple_of(r * BLOCK, BLOCK), BLOCK)] = hot
            return inner

        return lax.fori_loop(0, cells // BLOCK, band, carry)

    lax.fori_loop(0, nobs // OBS_CHUNK, build_pick, 0)

    def chunks(body):
        def run(c, carry):
            body(pl.ds(pl.multiple_of(c * CHUNK, CHUNK), CHUNK))
            return carry

        lax.fori_loop(0, cells // CHUNK, run, 0)

    def levels(g):
        return slice(g * GROUP, (g + 1) * GROUP)

    def member(m):
        return slice(m * GROUP, (m + 1) * GROUP)

    def project(g, rel, at):
        total = None
        for m in range(members):
            value = ens[rel, m, levels(g), at].astype(F32) * updates[g, member(m), at]
            total = value if total is None else total + value
        return total

    def arrive(dk):
        for dz in range(chips):
            rel = dk * chips + dz
            if rel:
                moved[rel].wait_recv()
            else:
                own.wait()

    at_a, at_b, at_c, at_o, at_d, at_g, at_t = {}, {}, {}, {}, {}, {}, {}

    def stage_a(i, g):
        if i == 0 and g == 0:
            arrive(1)

        def fill(at):
            for dz in range(chips):
                out_a[i, g, dz, :, at] = project(g, chips + dz, at)

        chunks(fill)
        at_a[i, g] = send(out_a.at[i, g], in_a.at[i, g], a_s.at[i, g], a_r.at[i, g], sibling)

    def stage_b(i, g):
        if i == 0 and g == 0:
            arrive(0)
        at_a[i, g].wait_recv()

        def fold(at):
            for dz in range(chips):
                sums[i, g, dz, :, at] = project(g, dz, at) + in_a[i, g, dz, :, at]

        chunks(fold)
        for dz in range(1, chips):
            at_b[i, g, dz] = send(
                sums.at[i, g, dz], in_b.at[i, g, dz - 1], b_s.at[i, g, dz - 1],
                b_r.at[i, g, dz - 1], {"slot": slot_at(-dz, 0)},
            )

    def stage_sum(i, g):
        for dz in range(1, chips):
            at_b[i, g, dz].wait_recv()
        total = sums[i, g, 0]
        for dz in range(1, chips):
            total = total + in_b[i, g, dz - 1]
        high, low = halves(total)
        pair[levels(g)] = high
        pair[LEV + g * GROUP : LEV + (g + 1) * GROUP] = low

    def observe_all():
        adjsum[...] = jnp.zeros_like(adjsum)

        def observe(q, carry):
            at = pl.ds(pl.multiple_of(q * OBS_CHUNK, OBS_CHUNK), OBS_CHUNK)
            table = pick[q]
            seen = dot(pair[...], table)
            seen = seen[:LEV] + seen[LEV:]
            w = wts[0, :, at]
            modelled = jnp.sum(w * seen, axis=0, keepdims=True)
            residual = inverse[:, at] * (modelled - innovation[:, at])
            up, down = halves(w * residual)
            back = dot_t(jnp.concatenate([up, down], axis=0), table)
            adjsum[...] += back[:LEV] + back[LEV:]
            return carry

        lax.fori_loop(0, nobs // OBS_CHUNK, observe, 0)

    def stage_c(i, g):
        adj[i, g, 0] = adjsum[levels(g)]
        for dz in range(1, chips):
            at_c[i, g, dz] = send(
                adj.at[i, g, 0], adj.at[i, g, dz], c_s.at[i, g, dz - 1], c_r.at[i, g, dz - 1],
                {"slot": slot_at(dz, 0)},
            )
        at_o[i, g] = send(
            adj.at[i, g, 0], adj.at[i, g, chips], o_s.at[i, g], o_r.at[i, g], sibling
        )

    def stage_d(i, g):
        for dz in range(1, chips):
            at_c[i, g, dz].wait_recv()
        at_d[i, g] = send(
            adj.at[i, g, pl.ds(1, chips - 1)], adj.at[i, g, pl.ds(chips + 1, chips - 1)],
            d_s.at[i, g], d_r.at[i, g], sibling,
        )

    def stage_force(i, g):
        at_o[i, g].wait_recv()
        at_d[i, g].wait_recv()

        def force(at):
            for m in range(members):
                total = ens[0, m, levels(g), at].astype(F32) * adj[i, g, 0, :, at]
                for rel in range(1, slots):
                    total = total + ens[rel, m, levels(g), at].astype(F32) * adj[i, g, rel, :, at]
                up, down = halves(total)
                forced[g, member(m), at] = up
                forced[g, part + m * GROUP : part + (m + 1) * GROUP, at] = down

        chunks(force)
        for d in range(1, spaces):
            to = space_at(d)
            both = dot(forced[g], dense[to])
            term[i, g, d - 1] = both[:part] + both[part:]
            at_t[i, g, d] = send(
                term.at[i, g, d - 1], term_in.at[i, g, d - 1], t_s.at[i, g, d - 1],
                t_r.at[i, g, d - 1], {"space": to},
            )
        both = dot(forced[g], dense[me])
        base[g] += both[:part] + both[part:]

    def stage_total(i, g):
        total = base[g]
        for d in range(1, spaces):
            at_t[i, g, d].wait_recv()
            total = total + term_in[i, g, d - 1]
        target = second_ref if i else first_ref
        for m in range(members):
            target[m * LEV + g * GROUP : m * LEV + (g + 1) * GROUP] = total[member(m)]
        if i == 0:
            for m in range(members):
                at = slice(m * LEV + g * GROUP, m * LEV + (g + 1) * GROUP)
                step[g, member(m)] = control[at].astype(F32) - descent_step * total[member(m)]
            for d in range(1, spaces):
                at_g[g, d] = send(
                    step.at[g], step_in.at[g, d - 1], g_s.at[g, d - 1], g_r.at[g, d - 1],
                    {"space": space_at(d)},
                )

    def spread(x, table):
        up, down = halves(x)
        both = dot_t(jnp.concatenate([up, down], axis=0), table)
        return both[:part] + both[part:]

    def stage_update(g):
        base[g] = step[g]
        updates[g] = spread(step[g], dense[me])
        for d in range(1, spaces):
            at_g[g, d].wait_recv()
            updates[g] += spread(step_in[g, d - 1], dense[space_at(-d)])

    value = dot_t(control[...], dense[me])
    for d in range(1, spaces):
        gathers[d - 1].wait_recv()
        value = value + dot_t(ctl_in[d - 1], dense[space_at(-d)])
    for g in range(groups):
        for m in range(members):
            at = slice(m * LEV + g * GROUP, m * LEV + (g + 1) * GROUP)
            updates[g, member(m)] = value[at]
            base[g, member(m)] = control[at].astype(F32)

    def on(stage, i):
        return functools.partial(stage, i)

    staged([on(stage_a, 0), on(stage_b, 0), on(stage_sum, 0)], groups)
    observe_all()
    for g in range(groups):
        stage_c(0, g)
    staged(
        [
            on(stage_d, 0), on(stage_force, 0), on(stage_total, 0), stage_update,
            on(stage_a, 1), on(stage_b, 1), on(stage_sum, 1),
        ],
        groups,
    )
    observe_all()
    for g in range(groups):
        stage_c(1, g)
    staged([on(stage_d, 1), on(stage_force, 1), on(stage_total, 1)], groups)
    for copy in started:
        copy.wait_send()


def per_device(control, block_lists, loc_tiles, ensemble, obs_col, obs_wts, innovation, inv_error):
    rows, width = control.shape
    cells = ensemble.shape[2]
    nobs = obs_col.shape[1]
    spaces, slots = lax.axis_size("space"), lax.axis_size("slot")
    chips = slots // CORES
    members = rows // LEV
    groups, part = LEV // GROUP, members * GROUP
    dma = pltpu.SemaphoreType.DMA
    vmem = pl.BlockSpec(memory_space=pltpu.VMEM)
    out = jax.ShapeDtypeStruct((rows, width), F32)
    return pl.pallas_call(
        functools.partial(kernel, spaces, slots),
        out_shape=(out, out),
        in_specs=[
            vmem, pl.BlockSpec(memory_space=pltpu.SMEM), vmem, pl.BlockSpec(memory_space=pl.ANY),
            vmem, vmem, vmem, vmem,
        ],
        out_specs=(vmem, vmem),
        scratch_shapes=[
            pltpu.VMEM((slots, members, LEV, cells), BF16),
            pltpu.VMEM((spaces, cells, width), BF16),
            pltpu.VMEM((nobs // OBS_CHUNK, cells, OBS_CHUNK), BF16),
            pltpu.VMEM((groups, part, cells), F32),
            pltpu.VMEM((2 * LEV, cells), BF16),
            pltpu.VMEM((LEV, cells), F32),
            pltpu.VMEM((groups, 2 * part, cells), BF16),
            pltpu.VMEM((2, groups, chips, GROUP, cells), F32),
            pltpu.VMEM((2, groups, chips, GROUP, cells), F32),
            pltpu.VMEM((2, groups, chips, GROUP, cells), F32),
            pltpu.VMEM((2, groups, chips - 1, GROUP, cells), F32),
            pltpu.VMEM((2, groups, slots, GROUP, cells), F32),
            pltpu.VMEM((2, groups, spaces - 1, part, width), F32),
            pltpu.VMEM((2, groups, spaces - 1, part, width), F32),
            pltpu.VMEM((groups, part, width), F32),
            pltpu.VMEM((groups, part, width), F32),
            pltpu.VMEM((spaces - 1, rows, width), BF16),
            pltpu.VMEM((groups, spaces - 1, part, width), F32),
            dma, dma((slots - 1,)), dma((slots - 1,)),
            dma((spaces - 1,)), dma((spaces - 1,)),
            dma((2, groups)), dma((2, groups)),
            dma((2, groups, chips - 1)), dma((2, groups, chips - 1)),
            dma((2, groups, chips - 1)), dma((2, groups, chips - 1)),
            dma((2, groups)), dma((2, groups)),
            dma((2, groups)), dma((2, groups)),
            dma((groups, spaces - 1)), dma((groups, spaces - 1)),
            dma((2, groups, spaces - 1)), dma((2, groups, spaces - 1)),
        ],
        compiler_params=pltpu.CompilerParams(
            collective_id=0, has_side_effects=True, vmem_limit_bytes=58 * 1024 * 1024
        ),
        name="envar_gradients",
    )(
        control, block_lists, loc_tiles, ensemble.reshape(slots, members, LEV, cells), obs_col,
        obs_wts, innovation, inv_error,
    )


def solution(mesh):
    placed = (
        P("slot", "space"),
        P("space", None),
        P("space", None, None, None),
        P("slot", None, "space"),
        P("slot", "space"),
        P("slot", None, "space"),
        P("slot", "space"),
        P("slot", "space"),
    )
    return jax.shard_map(
        per_device,
        mesh=mesh,
        in_specs=placed,
        out_specs=(P("slot", "space"), P("slot", "space")),
        check_vma=False,
    )
```

```python
import functools

import jax
import jax.numpy as jnp
from jax import lax
from jax.experimental import pallas as pl
from jax.experimental.pallas import tpu as pltpu
from jax.sharding import PartitionSpec as P

LEV = 48
BLOCK = 128
CORES = 2
CHUNK = 512
GROUP = 16
OBS_CHUNK = 512
descent_step = 0.5
F32 = jnp.float32
BF16 = jnp.bfloat16
MESH = pl.DeviceIdType.MESH


def halves(x):
    high = x.astype(BF16)
    return high, (x - high.astype(F32)).astype(BF16)


def dot(a, b):
    return lax.dot_general(a, b, (((1,), (0,)), ((), ())), preferred_element_type=F32)


def staged(stages, count):
    for tick in range(count + len(stages) - 1):
        for place in reversed(range(len(stages))):
            if 0 <= tick - place < count:
                stages[place](tick - place)


def kernel(
    spaces, slots,
    control, lists, tiles, ensemble, cols, wts, innovation, inverse,
    first_ref, second_ref,
    ens, dense, dense_t, pick, pick_t, updates, pair, adjsum, forced, out_a, in_a, sums, in_b, adj, term, term_in,
    base, step, ctl_in, step_in,
    local_sem, ens_s, ens_r, ctl_s, ctl_r, a_s, a_r, b_s, b_r, c_s, c_r, o_s, o_r, d_s, d_r,
    g_s, g_r, t_s, t_r,
):
    rows, width = control.shape
    members, cells = ensemble.shape[1], ensemble.shape[3]
    nobs = cols.shape[1]
    chips = slots // CORES
    part = members * GROUP
    groups = LEV // GROUP
    me = lax.axis_index("space")
    slot = lax.axis_index("slot")
    z, core = slot // CORES, lax.rem(slot, CORES)
    sibling = {"slot": slot + 1 - 2 * core}

    def slot_at(dz, dk):
        zz = lax.rem(z + dz + chips, chips)
        return zz * CORES + (core if dk == 0 else 1 - core)

    def space_at(d):
        return lax.rem(me + d + spaces, spaces)

    barrier = pltpu.get_barrier_semaphore()
    for dz in range(chips):
        for dk in range(CORES):
            if dz or dk:
                pl.semaphore_signal(
                    barrier, inc=1, device_id={"slot": slot_at(dz, dk)}, device_id_type=MESH
                )
    for d in range(1, spaces):
        pl.semaphore_signal(barrier, inc=1, device_id={"space": space_at(d)}, device_id_type=MESH)
    pl.semaphore_wait(barrier, slots - 1 + spaces - 1)

    started = []

    def send(src, dst, ssem, rsem, where):
        copy = pltpu.make_async_remote_copy(
            src_ref=src, dst_ref=dst, send_sem=ssem, recv_sem=rsem,
            device_id=where, device_id_type=MESH,
        )
        copy.start()
        started.append(copy)
        return copy

    gathers = [
        send(control, ctl_in.at[d - 1], ctl_s.at[d - 1], ctl_r.at[d - 1], {"space": space_at(d)})
        for d in range(1, spaces)
    ]
    moved = {}
    for dk in (1, 0):
        for dz in sorted(range(chips), key=lambda v: -min(v, chips - v)):
            if dz or dk:
                rel = dk * chips + dz
                to = slot_at(dz, dk)
                moved[rel] = send(
                    ensemble.at[to], ens.at[rel], ens_s.at[rel - 1], ens_r.at[rel - 1], {"slot": to}
                )
    own = pltpu.make_async_copy(ensemble.at[slot], ens.at[0], local_sem)
    own.start()

    per = width // BLOCK

    def build_dense(g, carry):
        one = lists[g, 0]
        two = lists[g, 1]
        tile_one = tiles[g, 0].astype(F32)
        tile_two = tiles[g, 1].astype(F32)
        flip_one, flip_two = tile_one.T, tile_two.T
        at = pl.ds(pl.multiple_of(g * BLOCK, BLOCK), BLOCK)
        for b in range(spaces * per):
            mask_one = jnp.where(one == b, 1.0, 0.0)
            mask_two = jnp.where(two == b, 1.0, 0.0)
            value = tile_one * mask_one + tile_two * mask_two
            dense[b // per, at, (b % per) * BLOCK : (b % per + 1) * BLOCK] = value.astype(BF16)
            value = flip_one * mask_one + flip_two * mask_two
            dense_t[b // per, (b % per) * BLOCK : (b % per + 1) * BLOCK, at] = value.astype(BF16)
        return carry

    lax.fori_loop(0, cells // BLOCK, build_dense, 0)

    first_cell = me * cells

    def build_pick(q, carry):
        line = cols[:, pl.ds(pl.multiple_of(q * OBS_CHUNK, OBS_CHUNK), OBS_CHUNK)] - first_cell

        def band(r, inner):
            rowid = lax.broadcasted_iota(jnp.int32, (BLOCK, OBS_CHUNK), 0) + r * BLOCK
            hot = jnp.where(rowid == line, 1.0, 0.0)
            at = pl.ds(pl.multiple_of(r * BLOCK, BLOCK), BLOCK)
            pick[q, at] = hot.astype(BF16)
            pick_t[q, :, at] = hot.T.astype(BF16)
            return inner

        return lax.fori_loop(0, cells // BLOCK, band, carry)

    lax.fori_loop(0, nobs // OBS_CHUNK, build_pick, 0)

    def chunks(body):
        def run(c, carry):
            body(pl.ds(pl.multiple_of(c * CHUNK, CHUNK), CHUNK))
            return carry

        lax.fori_loop(0, cells // CHUNK, run, 0)

    def levels(g):
        return slice(g * GROUP, (g + 1) * GROUP)

    def member(m):
        return slice(m * GROUP, (m + 1) * GROUP)

    def project(g, rel, at):
        total = None
        for m in range(members):
            value = ens[rel, m, levels(g), at].astype(F32) * updates[g, member(m), at]
            total = value if total is None else total + value
        return total

    def arrive(dk):
        for dz in range(chips):
            rel = dk * chips + dz
            if rel:
                moved[rel].wait_recv()
            else:
                own.wait()

    at_a, at_b, at_c, at_o, at_d, at_g, at_t = {}, {}, {}, {}, {}, {}, {}

    def stage_a(i, g):
        if i == 0 and g == 0:
            arrive(1)

        def fill(at):
            for dz in range(chips):
                out_a[i, g, dz, :, at] = project(g, chips + dz, at)

        chunks(fill)
        at_a[i, g] = send(out_a.at[i, g], in_a.at[i, g], a_s.at[i, g], a_r.at[i, g], sibling)

    def stage_b(i, g):
        if i == 0 and g == 0:
            arrive(0)
        at_a[i, g].wait_recv()

        def fold(at):
            for dz in range(chips):
                sums[i, g, dz, :, at] = project(g, dz, at) + in_a[i, g, dz, :, at]

        chunks(fold)
        for dz in range(1, chips):
            at_b[i, g, dz] = send(
                sums.at[i, g, dz], in_b.at[i, g, dz - 1], b_s.at[i, g, dz - 1],
                b_r.at[i, g, dz - 1], {"slot": slot_at(-dz, 0)},
            )

    def stage_sum(i, g):
        for dz in range(1, chips):
            at_b[i, g, dz].wait_recv()
        total = sums[i, g, 0]
        for dz in range(1, chips):
            total = total + in_b[i, g, dz - 1]
        high, low = halves(total)
        pair[levels(g)] = high
        pair[LEV + g * GROUP : LEV + (g + 1) * GROUP] = low

    def observe_all():
        adjsum[...] = jnp.zeros_like(adjsum)

        def observe(q, carry):
            at = pl.ds(pl.multiple_of(q * OBS_CHUNK, OBS_CHUNK), OBS_CHUNK)
            table = pick[q]
            seen = dot(pair[...], table)
            seen = seen[:LEV] + seen[LEV:]
            w = wts[0, :, at]
            modelled = jnp.sum(w * seen, axis=0, keepdims=True)
            residual = inverse[:, at] * (modelled - innovation[:, at])
            up, down = halves(w * residual)
            back = dot(jnp.concatenate([up, down], axis=0), pick_t[q])
            adjsum[...] += back[:LEV] + back[LEV:]
            return carry

        lax.fori_loop(0, nobs // OBS_CHUNK, observe, 0)

    def stage_c(i, g):
        adj[i, g, 0] = adjsum[levels(g)]
        for dz in range(1, chips):
            at_c[i, g, dz] = send(
                adj.at[i, g, 0], adj.at[i, g, dz], c_s.at[i, g, dz - 1], c_r.at[i, g, dz - 1],
                {"slot": slot_at(dz, 0)},
            )
        at_o[i, g] = send(
            adj.at[i, g, 0], adj.at[i, g, chips], o_s.at[i, g], o_r.at[i, g], sibling
        )

    def stage_d(i, g):
        for dz in range(1, chips):
            at_c[i, g, dz].wait_recv()
        at_d[i, g] = send(
            adj.at[i, g, pl.ds(1, chips - 1)], adj.at[i, g, pl.ds(chips + 1, chips - 1)],
            d_s.at[i, g], d_r.at[i, g], sibling,
        )

    def stage_force(i, g):
        at_o[i, g].wait_recv()
        at_d[i, g].wait_recv()

        def force(at):
            for m in range(members):
                total = ens[0, m, levels(g), at].astype(F32) * adj[i, g, 0, :, at]
                for rel in range(1, slots):
                    total = total + ens[rel, m, levels(g), at].astype(F32) * adj[i, g, rel, :, at]
                up, down = halves(total)
                forced[g, member(m), at] = up
                forced[g, part + m * GROUP : part + (m + 1) * GROUP, at] = down

        chunks(force)
        for d in range(1, spaces):
            to = space_at(d)
            both = dot(forced[g], dense[to])
            term[i, g, d - 1] = both[:part] + both[part:]
            at_t[i, g, d] = send(
                term.at[i, g, d - 1], term_in.at[i, g, d - 1], t_s.at[i, g, d - 1],
                t_r.at[i, g, d - 1], {"space": to},
            )
        both = dot(forced[g], dense[me])
        base[g] += both[:part] + both[part:]

    def stage_total(i, g):
        total = base[g]
        for d in range(1, spaces):
            at_t[i, g, d].wait_recv()
            total = total + term_in[i, g, d - 1]
        target = second_ref if i else first_ref
        for m in range(members):
            target[m * LEV + g * GROUP : m * LEV + (g + 1) * GROUP] = total[member(m)]
        if i == 0:
            for m in range(members):
                at = slice(m * LEV + g * GROUP, m * LEV + (g + 1) * GROUP)
                step[g, member(m)] = control[at].astype(F32) - descent_step * total[member(m)]
            for d in range(1, spaces):
                at_g[g, d] = send(
                    step.at[g], step_in.at[g, d - 1], g_s.at[g, d - 1], g_r.at[g, d - 1],
                    {"space": space_at(d)},
                )

    def spread(x, table):
        up, down = halves(x)
        both = dot(jnp.concatenate([up, down], axis=0), table)
        return both[:part] + both[part:]

    def stage_update(g):
        base[g] = step[g]
        updates[g] = spread(step[g], dense_t[me])
        for d in range(1, spaces):
            at_g[g, d].wait_recv()
            updates[g] += spread(step_in[g, d - 1], dense_t[space_at(-d)])

    value = dot(control[...], dense_t[me])
    for d in range(1, spaces):
        gathers[d - 1].wait_recv()
        value = value + dot(ctl_in[d - 1], dense_t[space_at(-d)])
    for g in range(groups):
        for m in range(members):
            at = slice(m * LEV + g * GROUP, m * LEV + (g + 1) * GROUP)
            updates[g, member(m)] = value[at]
            base[g, member(m)] = control[at].astype(F32)

    def on(stage, i):
        return functools.partial(stage, i)

    staged([on(stage_a, 0), on(stage_b, 0), on(stage_sum, 0)], groups)
    observe_all()
    staged(
        [
            on(stage_c, 0), on(stage_d, 0), on(stage_force, 0), on(stage_total, 0), stage_update,
            on(stage_a, 1), on(stage_b, 1), on(stage_sum, 1),
        ],
        groups,
    )
    observe_all()
    staged([on(stage_c, 1), on(stage_d, 1), on(stage_force, 1), on(stage_total, 1)], groups)
    for copy in started:
        copy.wait_send()


def per_device(control, block_lists, loc_tiles, ensemble, obs_col, obs_wts, innovation, inv_error):
    rows, width = control.shape
    cells = ensemble.shape[2]
    nobs = obs_col.shape[1]
    spaces, slots = lax.axis_size("space"), lax.axis_size("slot")
    chips = slots // CORES
    members = rows // LEV
    groups, part = LEV // GROUP, members * GROUP
    dma = pltpu.SemaphoreType.DMA
    vmem = pl.BlockSpec(memory_space=pltpu.VMEM)
    out = jax.ShapeDtypeStruct((rows, width), F32)
    return pl.pallas_call(
        functools.partial(kernel, spaces, slots),
        out_shape=(out, out),
        in_specs=[
            vmem, pl.BlockSpec(memory_space=pltpu.SMEM), vmem, pl.BlockSpec(memory_space=pl.ANY),
            vmem, vmem, vmem, vmem,
        ],
        out_specs=(vmem, vmem),
        scratch_shapes=[
            pltpu.VMEM((slots, members, LEV, cells), BF16),
            pltpu.VMEM((spaces, cells, width), BF16),
            pltpu.VMEM((spaces, width, cells), BF16),
            pltpu.VMEM((nobs // OBS_CHUNK, cells, OBS_CHUNK), BF16),
            pltpu.VMEM((nobs // OBS_CHUNK, OBS_CHUNK, cells), BF16),
            pltpu.VMEM((groups, part, cells), F32),
            pltpu.VMEM((2 * LEV, cells), BF16),
            pltpu.VMEM((LEV, cells), F32),
            pltpu.VMEM((groups, 2 * part, cells), BF16),
            pltpu.VMEM((2, groups, chips, GROUP, cells), F32),
            pltpu.VMEM((2, groups, chips, GROUP, cells), F32),
            pltpu.VMEM((2, groups, chips, GROUP, cells), F32),
            pltpu.VMEM((2, groups, chips - 1, GROUP, cells), F32),
            pltpu.VMEM((2, groups, slots, GROUP, cells), F32),
            pltpu.VMEM((2, groups, spaces - 1, part, width), F32),
            pltpu.VMEM((2, groups, spaces - 1, part, width), F32),
            pltpu.VMEM((groups, part, width), F32),
            pltpu.VMEM((groups, part, width), F32),
            pltpu.VMEM((spaces - 1, rows, width), BF16),
            pltpu.VMEM((groups, spaces - 1, part, width), F32),
            dma, dma((slots - 1,)), dma((slots - 1,)),
            dma((spaces - 1,)), dma((spaces - 1,)),
            dma((2, groups)), dma((2, groups)),
            dma((2, groups, chips - 1)), dma((2, groups, chips - 1)),
            dma((2, groups, chips - 1)), dma((2, groups, chips - 1)),
            dma((2, groups)), dma((2, groups)),
            dma((2, groups)), dma((2, groups)),
            dma((groups, spaces - 1)), dma((groups, spaces - 1)),
            dma((2, groups, spaces - 1)), dma((2, groups, spaces - 1)),
        ],
        compiler_params=pltpu.CompilerParams(
            collective_id=0, has_side_effects=True, vmem_limit_bytes=58 * 1024 * 1024
        ),
        name="envar_gradients",
    )(
        control, block_lists, loc_tiles, ensemble.reshape(slots, members, LEV, cells), obs_col,
        obs_wts, innovation, inv_error,
    )


def solution(mesh):
    placed = (
        P("slot", "space"),
        P("space", None),
        P("space", None, None, None),
        P("slot", None, "space"),
        P("slot", "space"),
        P("slot", None, "space"),
        P("slot", "space"),
        P("slot", "space"),
    )
    return jax.shard_map(
        per_device,
        mesh=mesh,
        in_specs=placed,
        out_specs=(P("slot", "space"), P("slot", "space")),
        check_vma=False,
    )
```
